32 devices in a mesh: batch: 4 (over z), tensor: 8 (over y, x, core).
Axes of the slice: x: 2, y: 2, z: 4, core: 2. Of those that a mesh axis runs over, the one named last changes fastest.
Arguments:
- attn_values: bfloat16 [1024, 8192], P('batch', 'tensor'), may hold values from -6 to 6
- out_weight: bfloat16 [8192, 8192], P('tensor'), may hold values from -0.09375 to 0.09375
- residual_t: bfloat16 [8192, 1024], P('tensor', 'batch'), may hold values from -6 to 6
- projector: bfloat16 [8192, 4096], P('tensor'), may hold values from -0.0625 to 0.0625
- student_input: bfloat16 [1024, 4096], P('batch', 'tensor'), may hold values from -6 to 6
- norm_gain: float32 [4096], replicated, may hold values from 0.1 to 1.9
- w_gate: bfloat16 [4096, 8192], P('batch', 'tensor'), may hold values from -0.09375 to 0.09375
- w_up: bfloat16 [4096, 8192], P('batch', 'tensor'), may hold values from -0.09375 to 0.09375
- w_down: bfloat16 [4096, 8192], P('batch', 'tensor'), may hold values from -0.0625 to 0.0625
- route_index: int32 [4, 64], P('batch'), may hold values from -1 to 255, as said below
Outputs:
- teacher_hidden: bfloat16 [8192, 1024], P('tensor', 'batch')
- grad_gate: float32 [4096, 8192], P('batch', 'tensor')
- grad_up: float32 [4096, 8192], P('batch', 'tensor')
- grad_down: float32 [4096, 8192], P('batch', 'tensor')
The draws below stay inside these ranges and needn't reach their ends.
Inputs may be any that keep to these rules, and one draw needn't show every extreme that they name: `route_index`: in each batch group the live slots come first, hold distinct positions in increasing order, and the empty slots after them hold -1. The batch groups hold 128 live slots together, and some batch group has all 64 slots live.
All inputs are finite; a program needn't handle non-finite values.
Results may differ from the reference program's by a relative error of at most 0.025.
Values may be sent and summed in bfloat16 or wider, within the bound.
A program may use at most 128 MiB of HBM per device.

```python
import math
import jax
import jax.numpy as jnp
from jax import lax

DT = 8192
D = 4096
FF = 8192
TOK = 256
CAP = 32
CAPMAX = 64
ROUTED = 128
TOKENS = 1024
N_BATCH = 4
N_TENSOR = 8


def draw_route_index(key, part):
    key_perm, key_spread, key_pos = jax.random.split(jax.random.fold_in(key, 71), 3)
    half_groups = N_BATCH // 2
    spread = jax.random.randint(key_spread, (half_groups,), 0, CAP + 1)
    spread = spread.at[0].set(CAP)
    counts = jnp.concatenate([CAP + spread, CAP - spread])
    order_groups = jax.random.permutation(key_perm, N_BATCH)
    counts = counts[order_groups]
    group_keys = jax.random.split(key_pos, N_BATCH)

    def one_group(group_key, live_count):
        shuffled = jax.random.permutation(group_key, TOK)[:CAPMAX]
        slot_ids = jnp.arange(CAPMAX, dtype=jnp.int32)
        chosen = jnp.where(slot_ids < live_count, shuffled, TOK)
        chosen = jnp.sort(chosen)
        return jnp.where(slot_ids < live_count, chosen, -1)
    return jax.vmap(one_group)(group_keys, counts).astype(jnp.int32)


def raised(array, stream_key, source, target, blocks, factor):
    owner, partner = [(jnp.arange(array.shape[dim]) // (array.shape[dim] // blocks)).reshape([-1 if axis == dim else 1 for axis in range(array.ndim)]) for dim in (source, target)]
    chosen = jax.random.permutation(stream_key, blocks)[partner]
    strong = (owner == chosen) | (owner == (partner + blocks // 2) % blocks)
    return jnp.where(strong, factor * array, array)


def steps_of(key, shape, shards, least, high):
    loudness, own = 1.0, jax.random.fold_in(key, 6)
    for position, shards_of in shards:
        heights = jnp.exp(jax.random.uniform(jax.random.fold_in(own, position), (shards_of,), jnp.float32, least / len(shards), high / len(shards)))
        loudness = loudness * jnp.repeat(heights, shape[position] // shards_of).reshape([-1 if axis == position else 1 for axis in range(len(shape))])
    return loudness


def bell_draw(own_key, shape, deviation, reach, cuts=(), kind=jnp.bfloat16):
    level = steps_of(own_key, shape, cuts, -0.22, 0.18) if cuts else 1.0
    values = jax.random.normal(own_key, shape, jnp.float32) * deviation * level
    return jnp.minimum(jnp.maximum(values, -reach), reach).astype(kind)


def gaussian_with(own_key, extent, scale, limit, shards, heavy, kind=jnp.bfloat16):
    drawn = scale * jax.random.normal(own_key, extent, jnp.float32)
    if shards:
        drawn = drawn * steps_of(own_key, extent, shards, -0.22, 0.18)
    return jnp.clip(raised(drawn, jax.random.fold_in(own_key, 3), *heavy), -limit, limit).astype(kind)


def setup_inputs(seed: int = 0) -> dict:
    arg_keys = jax.random.split(jax.random.key(seed), 11)
    attn_values = bell_draw(arg_keys[0], (TOKENS, DT), 1.0, 6.0, ((0, 4), (1, 8)))
    out_weight = gaussian_with(arg_keys[1], (DT, DT), DT ** -0.5, 0.09375, ((0, 8),), (0, 1, 8, 2.0))
    residual_t = bell_draw(arg_keys[2], (DT, TOKENS), 1.0, 6.0, ((0, 8), (1, 4)))
    projector = bell_draw(arg_keys[3], (DT, D), DT ** -0.5, 0.0625, ((0, 8),))
    student_input = bell_draw(arg_keys[4], (TOKENS, D), 1.0, 6.0, ((0, 4), (1, 8)))
    norm_gain = jnp.clip(1.0 + 0.18 * jax.random.normal(arg_keys[5], (D,), jnp.float32), 0.1, 1.9)
    w_gate = bell_draw(arg_keys[6], (D, FF), D ** -0.5, 0.09375, ((0, 4), (1, 8)))
    w_up = bell_draw(arg_keys[7], (D, FF), D ** -0.5, 0.09375, ((0, 4), (1, 8)))
    w_down = bell_draw(arg_keys[8], (D, FF), FF ** -0.5, 0.0625, ((0, 4), (1, 8)))
    route_index = draw_route_index(jax.random.fold_in(arg_keys[10], 71), 0)
    return {"attn_values": attn_values, "out_weight": out_weight, "residual_t": residual_t, "projector": projector, "student_input": student_input, "norm_gain": norm_gain, "w_gate": w_gate, "w_up": w_up, "w_down": w_down, "route_index": route_index}


epsilon = 1e-05

def reference(attn_values, out_weight, residual_t, projector, student_input, norm_gain, w_gate, w_up, w_down, route_index):
    shard_width = DT // N_TENSOR

    def teacher_step(running, shard_no):
        offset = (shard_no * shard_width).astype(jnp.int32)
        columns = lax.dynamic_slice_in_dim(attn_values, offset, shard_width, 1)
        rows_block = lax.dynamic_slice_in_dim(out_weight, offset, shard_width, 0)
        partial_sum = lax.dot_general(rows_block, columns, (((0,), (1,)), ((), ())), preferred_element_type=jnp.float32)
        rounded = lax.optimization_barrier(partial_sum.astype(jnp.bfloat16))
        return (running + rounded.astype(jnp.float32), None)
    summed, _ = lax.scan(teacher_step, jnp.zeros((DT, TOKENS), jnp.float32), jnp.arange(N_TENSOR, dtype=jnp.int32))
    teacher_hidden = (residual_t.astype(jnp.float32) + summed).astype(jnp.bfloat16)
    loss_scale = 1.0 / math.sqrt(ROUTED)

    def group_step(running, group_no):
        slot_pos = lax.dynamic_index_in_dim(route_index, group_no, 0, keepdims=False)
        present = slot_pos >= 0
        safe_slot = (jnp.maximum(slot_pos, 0) + group_no * TOK).astype(jnp.int32)
        routed_teacher = jnp.where(present[None, :], jnp.take(teacher_hidden, safe_slot, axis=1), 0).astype(jnp.bfloat16)
        target = lax.dot_general(routed_teacher, projector, (((0,), (0,)), ((), ())), preferred_element_type=jnp.float32)
        routed_input = jnp.where(present[:, None], jnp.take(student_input, safe_slot, axis=0), 0).astype(jnp.float32)
        mean_square = lax.optimization_barrier(jnp.mean(routed_input * routed_input, axis=1, keepdims=True))
        normed = (routed_input * lax.rsqrt(mean_square + epsilon) * norm_gain[None, :]).astype(jnp.bfloat16)
        gate_act = jnp.dot(normed, w_gate, preferred_element_type=jnp.float32)
        up_act = jnp.dot(normed, w_up, preferred_element_type=jnp.float32)
        sigma_gate = jax.nn.sigmoid(gate_act)
        hidden = (gate_act * sigma_gate * up_act).astype(jnp.bfloat16)
        student_out = lax.dot_general(hidden, w_down, (((1,), (1,)), ((), ())), preferred_element_type=jnp.float32)
        misfit = jnp.where(present[:, None], student_out - target, 0.0)
        grad_out = (misfit * loss_scale).astype(jnp.bfloat16)
        grad_hidden = jnp.dot(grad_out, w_down, preferred_element_type=jnp.float32)
        grad_gate_act = (grad_hidden * up_act * sigma_gate * (1.0 + gate_act * (1.0 - sigma_gate))).astype(jnp.bfloat16)
        grad_up_act = (grad_hidden * gate_act * sigma_gate).astype(jnp.bfloat16)
        dims = (((0,), (0,)), ((), ()))
        gate_part = lax.dot_general(normed, grad_gate_act, dims, preferred_element_type=jnp.float32)
        up_part = lax.dot_general(normed, grad_up_act, dims, preferred_element_type=jnp.float32)
        down_part = lax.dot_general(grad_out, hidden, dims, preferred_element_type=jnp.float32)
        parts = (gate_part, up_part, down_part)
        updated = tuple((acc + lax.optimization_barrier(part.astype(jnp.bfloat16)).astype(jnp.float32) for acc, part in zip(running, parts)))
        return (updated, None)
    zero_grad = jnp.zeros((D, FF), jnp.float32)
    grads, _ = lax.scan(group_step, (zero_grad, zero_grad, zero_grad), jnp.arange(N_BATCH, dtype=jnp.int32))
    return (teacher_hidden, grads[0], grads[1], grads[2])
```

```python
import math

import jax
import jax.numpy as jnp
from jax import lax
from jax.sharding import PartitionSpec as P

epsilon = 1e-05
f32 = jnp.float32
bf16 = jnp.bfloat16


def contract(left, right, left_dim, right_dim):
    return lax.dot_general(
        left, right, (((left_dim,), (right_dim,)), ((), ())), preferred_element_type=f32
    )


def on_device(
    attn_values,
    out_weight,
    residual_t,
    projector,
    student_input,
    norm_gain,
    w_gate,
    w_up,
    w_down,
    route_index,
):
    group_count = lax.axis_size("batch")
    mean_routed = student_input.shape[0] // 8
    routed = mean_routed * group_count
    loss_scale = 1.0 / math.sqrt(routed)

    every_route = lax.all_gather(route_index, "batch", axis=0, tiled=True).reshape(-1)
    live = every_route >= 0
    rank = jnp.cumsum(live.astype(jnp.int32)) - 1
    row_ids = lax.broadcasted_iota(jnp.int32, (routed, live.shape[0]), 0)
    select = ((rank[None, :] == row_ids) & live[None, :]).astype(bf16)
    live_row = lax.broadcasted_iota(jnp.int32, (routed, 1), 0) <= rank[-1]

    slot_pos = route_index[0]
    present = slot_pos >= 0
    safe_slot = jnp.maximum(slot_pos, 0)
    local_rows = jnp.where(present[:, None], jnp.take(student_input, safe_slot, axis=0), 0)
    routed_input = lax.all_gather(local_rows, "tensor", axis=1, tiled=True).astype(f32)
    mean_square = jnp.mean(routed_input * routed_input, axis=1, keepdims=True)
    normed = (routed_input * lax.rsqrt(mean_square + epsilon) * norm_gain[None, :]).astype(bf16)
    every_normed = lax.all_to_all(normed, "batch", split_axis=1, concat_axis=0, tiled=True)

    summed = lax.psum_scatter(
        contract(out_weight, attn_values, 0, 1).astype(bf16),
        "tensor",
        scatter_dimension=0,
        tiled=True,
    ).astype(f32)
    teacher_hidden = (residual_t.astype(f32) + summed).astype(bf16)

    rows = contract(select, every_normed, 1, 0).astype(bf16)
    gate_up = lax.psum(
        jnp.stack([contract(rows, w_gate, 1, 0), contract(rows, w_up, 1, 0)]).astype(bf16),
        "batch",
    ).astype(f32)
    gate_act, up_act = gate_up[0], gate_up[1]
    sigma_gate = jax.nn.sigmoid(gate_act)
    hidden = (gate_act * sigma_gate * up_act).astype(bf16)
    out_part = contract(hidden, w_down, 1, 1)

    routed_teacher = jnp.where(present[None, :], jnp.take(teacher_hidden, safe_slot, axis=1), 0)
    target_part = contract(routed_teacher, projector, 0, 0).astype(bf16)
    every_target = lax.all_to_all(target_part, "batch", split_axis=1, concat_axis=0, tiled=True)
    target_rows = contract(select, every_target, 1, 0)

    misfit = lax.psum((out_part - target_rows).astype(bf16), "tensor").astype(f32)
    grad_out = (jnp.where(live_row, misfit, 0.0) * loss_scale).astype(bf16)
    grad_hidden = lax.psum(contract(grad_out, w_down, 1, 0).astype(bf16), "batch").astype(f32)
    grad_gate_act = (
        grad_hidden * up_act * sigma_gate * (1.0 + gate_act * (1.0 - sigma_gate))
    ).astype(bf16)
    grad_up_act = (grad_hidden * gate_act * sigma_gate).astype(bf16)
    grad_gate = contract(rows, grad_gate_act, 0, 0)
    grad_up = contract(rows, grad_up_act, 0, 0)
    grad_down = contract(grad_out, hidden, 0, 0)
    return (teacher_hidden, grad_gate, grad_up, grad_down)


def solution(mesh):
    in_specs = (
        P("batch", "tensor"),
        P("tensor", None),
        P("tensor", "batch"),
        P("tensor", None),
        P("batch", "tensor"),
        P(),
        P("batch", "tensor"),
        P("batch", "tensor"),
        P("batch", "tensor"),
        P("batch", None),
    )
    out_specs = (
        P("tensor", "batch"),
        P("batch", "tensor"),
        P("batch", "tensor"),
        P("batch", "tensor"),
    )
    return jax.shard_map(
        on_device, mesh=mesh, in_specs=in_specs, out_specs=out_specs, check_vma=False
    )
```

```python
import functools
import math

import jax
import jax.numpy as jnp
from jax import lax
from jax.experimental import pallas as pl
from jax.experimental.pallas import tpu as pltpu
from jax.sharding import PartitionSpec as P

epsilon = 1e-05
f32 = jnp.float32
bf16 = jnp.bfloat16


def contract(left, right, left_dim, right_dim):
    return lax.dot_general(
        left, right, (((left_dim,), (right_dim,)), ((), ())), preferred_element_type=f32
    )


VMEM = pl.BlockSpec(memory_space=pltpu.VMEM)


def meet(axis, size):
    me = lax.axis_index(axis)
    barrier = pltpu.get_barrier_semaphore()
    for step in range(1, size):
        pl.semaphore_signal(
            barrier,
            inc=1,
            device_id={axis: lax.rem(me + step, size)},
            device_id_type=pl.DeviceIdType.MESH,
        )
    pl.semaphore_wait(barrier, size - 1)
    return me


def send(source, land, send_sem, recv_sem, axis, size, me):
    copies = []
    for step in range(1, size):
        peer = lax.rem(me + step, size)
        copy = pltpu.make_async_remote_copy(
            src_ref=source(peer),
            dst_ref=land.at[step - 1],
            send_sem=send_sem.at[step - 1],
            recv_sem=recv_sem.at[step - 1],
            device_id={axis: peer},
            device_id_type=pl.DeviceIdType.MESH,
        )
        copy.start()
        copies.append(copy)
    return copies


def exchange_kernel(axis, size, gather, x, out, land, send_sem, recv_sem):
    me = meet(axis, size)
    source = (lambda peer: x) if gather else (lambda peer: x.at[peer])
    copies = send(source, land, send_sem, recv_sem, axis, size, me)
    out[me] = x[...] if gather else x[me]
    for step in range(1, size):
        copies[step - 1].wait()
        out[lax.rem(me + size - step, size)] = land[step - 1]


def sum_kernel(axis, size, scale, x, out, land, share, late, sems):
    me = meet(axis, size)
    first = send(lambda peer: x.at[peer], land, sems.at[0], sems.at[1], axis, size, me)
    total = x[me].astype(f32)
    for step in range(1, size):
        first[step - 1].wait()
        total = total + land[step - 1].astype(f32)
    share[...] = (total * scale).astype(bf16)
    second = send(lambda peer: share, late, sems.at[2], sems.at[3], axis, size, me)
    out[me] = share[...]
    for step in range(1, size):
        second[step - 1].wait()
        out[lax.rem(me + size - step, size)] = late[step - 1]


def exchange(x, axis, ident, gather=False):
    size = lax.axis_size(axis)
    block = x.shape if gather else x.shape[1:]
    return pl.pallas_call(
        functools.partial(exchange_kernel, axis, size, gather),
        out_shape=jax.ShapeDtypeStruct((size,) + block, x.dtype),
        in_specs=[VMEM],
        out_specs=VMEM,
        scratch_shapes=[
            pltpu.VMEM((size - 1,) + block, x.dtype),
            pltpu.SemaphoreType.DMA((size - 1,)),
            pltpu.SemaphoreType.DMA((size - 1,)),
        ],
        compiler_params=pltpu.CompilerParams(collective_id=ident, has_side_effects=True),
    )(x)


def all_sum(terms, axis, ident, scale=1.0):
    size = lax.axis_size(axis)
    shares = terms.reshape((size, terms.shape[0] // size) + terms.shape[1:])
    block = shares.shape[1:]
    return pl.pallas_call(
        functools.partial(sum_kernel, axis, size, scale),
        out_shape=jax.ShapeDtypeStruct(shares.shape, bf16),
        in_specs=[VMEM],
        out_specs=VMEM,
        scratch_shapes=[
            pltpu.VMEM((size - 1,) + block, bf16),
            pltpu.VMEM(block, bf16),
            pltpu.VMEM((size - 1,) + block, bf16),
            pltpu.SemaphoreType.DMA((4, size - 1)),
        ],
        compiler_params=pltpu.CompilerParams(collective_id=ident, has_side_effects=True),
    )(shares).reshape(terms.shape)


def on_device(
    attn_values,
    out_weight,
    residual_t,
    projector,
    student_input,
    norm_gain,
    w_gate,
    w_up,
    w_down,
    route_index,
):
    group_count = lax.axis_size("batch")
    mean_routed = student_input.shape[0] // 8
    routed = mean_routed * group_count
    loss_scale = 1.0 / math.sqrt(routed)

    every_route = exchange(
        jnp.pad(route_index, ((0, 7), (0, -route_index.shape[1] % 128)), constant_values=-1),
        "batch",
        1,
        gather=True,
    )[:, 0, : route_index.shape[1]].reshape(-1)
    live = every_route >= 0
    rank = jnp.cumsum(live.astype(jnp.int32)) - 1
    row_ids = lax.broadcasted_iota(jnp.int32, (routed, live.shape[0]), 0)
    select = ((rank[None, :] == row_ids) & live[None, :]).astype(bf16)
    live_row = lax.broadcasted_iota(jnp.int32, (routed, 1), 0) <= rank[-1]

    slot_pos = route_index[0]
    present = slot_pos >= 0
    safe_slot = jnp.maximum(slot_pos, 0)
    local_rows = jnp.where(present[:, None], jnp.take(student_input, safe_slot, axis=0), 0)
    routed_input = exchange(local_rows, "tensor", 2, gather=True).astype(f32)
    width = routed_input.shape[0] * routed_input.shape[2]
    mean_square = jnp.sum(routed_input * routed_input, axis=(0, 2), keepdims=True) / width
    gain = norm_gain.reshape(routed_input.shape[0], 1, -1)
    normed = (routed_input * lax.rsqrt(mean_square + epsilon) * gain).astype(bf16)
    normed = jnp.swapaxes(normed, 0, 1).reshape(slot_pos.shape[0], group_count, -1)
    every_normed = exchange(jnp.swapaxes(normed, 0, 1), "batch", 3)
    every_normed = every_normed.reshape(live.shape[0], -1)

    summed = lax.psum_scatter(
        contract(out_weight, attn_values, 0, 1).astype(bf16),
        "tensor",
        scatter_dimension=0,
        tiled=True,
    ).astype(f32)
    teacher_hidden = (residual_t.astype(f32) + summed).astype(bf16)

    rows = contract(select, every_normed, 1, 0).astype(bf16)
    gate_up = jnp.concatenate([contract(rows, w_gate, 1, 0), contract(rows, w_up, 1, 0)])
    gate_up = all_sum(gate_up.astype(bf16), "batch", 4).astype(f32)
    gate_act, up_act = gate_up[:routed], gate_up[routed:]
    sigma_gate = jax.nn.sigmoid(gate_act)
    hidden = (gate_act * sigma_gate * up_act).astype(bf16)
    out_part = contract(hidden, w_down, 1, 1)

    routed_teacher = jnp.where(present[None, :], jnp.take(teacher_hidden, safe_slot, axis=1), 0)
    target_part = contract(routed_teacher, projector, 0, 0).astype(bf16)
    target_part = target_part.reshape(slot_pos.shape[0], group_count, -1)
    every_target = exchange(jnp.swapaxes(target_part, 0, 1), "batch", 5)
    every_target = every_target.reshape(live.shape[0], -1)
    target_rows = contract(select, every_target, 1, 0)

    misfit = jnp.where(live_row, out_part - target_rows, 0.0)
    grad_out = all_sum(misfit.astype(bf16), "tensor", 6, loss_scale)
    grad_hidden = all_sum(contract(grad_out, w_down, 1, 0).astype(bf16), "batch", 7).astype(f32)
    grad_gate_act = (
        grad_hidden * up_act * sigma_gate * (1.0 + gate_act * (1.0 - sigma_gate))
    ).astype(bf16)
    grad_up_act = (grad_hidden * gate_act * sigma_gate).astype(bf16)
    grad_gate = contract(rows, grad_gate_act, 0, 0)
    grad_up = contract(rows, grad_up_act, 0, 0)
    grad_down = contract(grad_out, hidden, 0, 0)
    return (teacher_hidden, grad_gate, grad_up, grad_down)


def solution(mesh):
    in_specs = (
        P("batch", "tensor"),
        P("tensor", None),
        P("tensor", "batch"),
        P("tensor", None),
        P("batch", "tensor"),
        P(),
        P("batch", "tensor"),
        P("batch", "tensor"),
        P("batch", "tensor"),
        P("batch", None),
    )
    out_specs = (
        P("tensor", "batch"),
        P("batch", "tensor"),
        P("batch", "tensor"),
        P("batch", "tensor"),
    )
    return jax.shard_map(
        on_device, mesh=mesh, in_specs=in_specs, out_specs=out_specs, check_vma=False
    )
```
